128 devices in a mesh: ctx: 8 (over z, x_hi), head: 16 (over y, x_lo, core).
Axes of the slice: x: 4 (x_hi: 2, x_lo: 2; x = x_hi * 2 + x_lo), y: 4, z: 4, core: 2. Of those that a mesh axis runs over, the one named last changes fastest.
Arguments:
- video: bfloat16 [6144, 4096], P('ctx', 'head'), may hold values from -6 to 6
- audio: bfloat16 [768, 2048], P('ctx', 'head'), may hold values from -6 to 6
- video_gain: float32 [4096], P('head'), may hold values from 0.1 to 1.9
- audio_gain: float32 [2048], P('head'), may hold values from 0.1 to 1.9
- video_qkv: bfloat16 [4096, 3, 4096], P(None, None, 'head'), as said below
- video_cross: bfloat16 [4096, 3, 2048], P(None, None, 'head'), as said below
- audio_cross: bfloat16 [2048, 3, 2048], P(None, None, 'head'), as said below
- video_out: bfloat16 [4096, 4096], P('head'), may hold values from -0.09375 to 0.09375
- cross_video_out: bfloat16 [2048, 4096], P('head'), may hold values from -0.125 to 0.125
- cross_audio_out: bfloat16 [2048, 2048], P('head'), may hold values from -0.125 to 0.125
Outputs:
- video_result: bfloat16 [6144, 4096], P('ctx', 'head')
- audio_result: bfloat16 [768, 2048], P('ctx', 'head')
The draws below stay inside these ranges and needn't reach their ends.
Inputs may be any that keep to these rules, and one draw needn't show every extreme that they name: `video_qkv`: entries lie within -32 / sqrt(4096) and 32 / sqrt(4096). `video_cross`: entries lie within -32 / sqrt(4096) and 32 / sqrt(4096). `audio_cross`: entries lie within -32 / sqrt(2048) and 32 / sqrt(2048).
All inputs are finite; a program needn't handle non-finite values.
Results may differ from the reference program's by a relative error of at most 0.014.
The reference program's roundings to bfloat16 on the way count: a program that leaves them out, or rounds other values in their place, can miss the bound.
Values may be sent and summed in bfloat16 or wider, within the bound.
No kernel may reach another device: no remote copies, remote signals or barrier semaphores. Data moves between devices by JAX's collectives and lax.ppermute only.
A program may use at most 128 MiB of HBM per device.

```python
import jax
import jax.numpy as jnp
from jax import lax

DV = 4096
DA = 2048
DC = 2048
HD = 128
VTOK = 6144
ATOK = 768


def projection_draw(key, element_salt, heads_salt, rows, width):
    element_key = jax.random.fold_in(key, element_salt)
    heads = width // HD
    flags = (jax.random.permutation(jax.random.fold_in(key, heads_salt), heads) < max(1, heads // 4)).astype(jnp.float32)
    factor = 8.0
    base = jax.random.truncated_normal(element_key, -4.0, 4.0, (rows, 3, width), jnp.float32)
    columns = jnp.repeat(1.0 + (factor - 1.0) * flags, HD)
    blocks = jnp.array([1.0, 1.0, 0.0], jnp.float32)
    scaling = 1.0 + blocks[:, None] * (columns[None, :] - 1.0)
    return (base * scaling[None, :, :] * rows ** (-0.5)).astype(jnp.bfloat16)


def draw_video_qkv(key, part):
    return projection_draw(key, 11, 21, DV, DV)


def draw_video_cross(key, part):
    return projection_draw(key, 12, 22, DV, DC)


def draw_audio_cross(key, part):
    return projection_draw(key, 13, 22, DA, DC)


def level_of(own_key, shape, pieces, low, largest):
    loudness = 1.0
    for dim, shards_of in pieces:
        draws = jax.random.uniform(jax.random.fold_in(jax.random.fold_in(own_key, 6), dim), (shards_of,), jnp.float32, low / len(pieces), largest / len(pieces))
        loudness = loudness * jnp.repeat(jnp.exp(draws), shape[dim] // shards_of).reshape((-1,) + (1,) * (len(shape) - 1 - dim))
    return loudness


def bell_draw(own_key, dims, scale, most, pieces=(), held_as=jnp.bfloat16):
    values = scale * jax.random.normal(own_key, dims, jnp.float32)
    if pieces:
        values = values * level_of(own_key, dims, pieces, -0.22, 0.18)
    return jnp.clip(values, -most, most).astype(held_as)


def setup_inputs(seed: int = 0) -> dict:
    key_list = jax.random.split(jax.random.key(seed), 11)
    video = bell_draw(key_list[0], (VTOK, DV), 1.0, 6.0, ((0, 8), (1, 16)))
    audio = bell_draw(key_list[1], (ATOK, DA), 1.0, 6.0, ((0, 8), (1, 16)))
    video_gain = jnp.clip(1.0 + 0.18 * jax.random.normal(key_list[2], (DV,), jnp.float32), 0.1, 1.9)
    audio_gain = jnp.clip(1.0 + 0.18 * jax.random.normal(key_list[3], (DA,), jnp.float32), 0.1, 1.9)
    video_qkv = draw_video_qkv(jax.random.fold_in(key_list[10], 71), 0)
    video_cross = draw_video_cross(jax.random.fold_in(key_list[10], 71), 0)
    audio_cross = draw_audio_cross(jax.random.fold_in(key_list[10], 71), 0)
    video_out = bell_draw(key_list[7], (DV, DV), DV ** -0.5, 0.09375, ((0, 16),))
    cross_video_out = bell_draw(key_list[8], (DC, DV), DC ** -0.5, 0.125, ((0, 16),))
    cross_audio_out = bell_draw(key_list[9], (DC, DA), DC ** -0.5, 0.125, ((0, 16),))
    return dict(video=video, audio=audio, video_gain=video_gain, audio_gain=audio_gain, video_qkv=video_qkv, video_cross=video_cross, audio_cross=audio_cross, video_out=video_out, cross_video_out=cross_video_out, cross_audio_out=cross_audio_out)


EPSILON = 1e-06

def attend(queries, keys, values):
    heads = queries.shape[1] // HD
    scale = HD ** (-0.5)

    def split_heads(matrix):
        return matrix.reshape(matrix.shape[0], heads, HD).transpose(1, 0, 2)

    def one_head(operands):
        query_block, key_block, value_block = operands
        scores = jnp.dot(query_block, key_block.T, preferred_element_type=jnp.float32) * scale
        highest = lax.optimization_barrier(jnp.max(scores, axis=1, keepdims=True))
        weights = jnp.exp(scores - highest)
        totals = lax.optimization_barrier(jnp.sum(weights, axis=1, keepdims=True))
        return jnp.dot(weights.astype(jnp.bfloat16), value_block, preferred_element_type=jnp.float32) / totals
    blocks = lax.map(one_head, (split_heads(queries), split_heads(keys), split_heads(values)))
    return blocks.transpose(1, 0, 2).reshape(queries.shape[0], heads * HD).astype(jnp.bfloat16)

def reference(video, audio, video_gain, audio_gain, video_qkv, video_cross, audio_cross, video_out, cross_video_out, cross_audio_out):
    video_wide = video.astype(jnp.float32)
    audio_wide = audio.astype(jnp.float32)
    video_rate = lax.rsqrt(lax.optimization_barrier(jnp.sum(video_wide * video_wide, axis=1)) / DV + EPSILON)
    audio_rate = lax.rsqrt(lax.optimization_barrier(jnp.sum(audio_wide * audio_wide, axis=1)) / DA + EPSILON)
    video_scaled = (video_wide * video_gain).astype(jnp.bfloat16)
    audio_scaled = (audio_wide * audio_gain).astype(jnp.bfloat16)
    self_proj = (jnp.dot(video_scaled, video_qkv.reshape(DV, 3 * DV), preferred_element_type=jnp.float32) * video_rate[:, None]).astype(jnp.bfloat16)
    video_mixed = (jnp.dot(video_scaled, video_cross.reshape(DV, 3 * DC), preferred_element_type=jnp.float32) * video_rate[:, None]).astype(jnp.bfloat16)
    audio_mixed = (jnp.dot(audio_scaled, audio_cross.reshape(DA, 3 * DC), preferred_element_type=jnp.float32) * audio_rate[:, None]).astype(jnp.bfloat16)
    self_out = attend(self_proj[:, :DV], self_proj[:, DV:2 * DV], self_proj[:, 2 * DV:])
    video_cross_out = attend(video_mixed[:, :DC], audio_mixed[:, DC:2 * DC], audio_mixed[:, 2 * DC:])
    audio_cross_out = attend(audio_mixed[:, :DC], video_mixed[:, DC:2 * DC], video_mixed[:, 2 * DC:])
    video_sum = jnp.dot(self_out, video_out, preferred_element_type=jnp.float32) + jnp.dot(video_cross_out, cross_video_out, preferred_element_type=jnp.float32)
    audio_sum = jnp.dot(audio_cross_out, cross_audio_out, preferred_element_type=jnp.float32)
    return ((video_wide + video_sum).astype(jnp.bfloat16), (audio_wide + audio_sum).astype(jnp.bfloat16))
```

```python
import functools
import math

import jax
import jax.numpy as jnp
from jax import lax
from jax.experimental import pallas as pl
from jax.experimental.pallas import tpu as pltpu
from jax.sharding import Mesh, PartitionSpec as P

HD = 128
EPSILON = 1e-06
SCALE = HD**-0.5
HEAD = ("y", "xl", "c")
CTX = ("z", "xh")
HALVES = 2
BF = jnp.bfloat16
F32 = jnp.float32
MEGA = 1 << 20
NT = (((1,), (1,)), ((), ()))


def shift(axis, by):
    n = lax.axis_size(axis)
    return [(i, (i + by) % n) for i in range(n)]


def sent_by(x, axis, by=1):
    return lax.ppermute(x, axis, shift(axis, by))


def sent_to_all(x, axes):
    n = math.prod(lax.axis_size(a) for a in axes)
    copies = jnp.broadcast_to(x, (n, *x.shape))
    return lax.all_to_all(copies, axes, split_axis=0, concat_axis=0, tiled=True)


def params(limit_mb):
    return pltpu.CompilerParams(vmem_limit_bytes=limit_mb * MEGA)


def cost(flops, moved, exps=0):
    return pl.CostEstimate(flops=int(flops), bytes_accessed=int(moved), transcendentals=int(exps))


def gather_chunks(table, chunk_refs, x, sems):
    width = chunk_refs[0].shape[1]
    copies = []
    for k, chunk in enumerate(chunk_refs):
        at = pl.multiple_of(table[1 + k] * width, width)
        copies.append(pltpu.make_async_copy(chunk, x.at[:, pl.ds(at, width)], sems.at[k]))
    for copy in copies:
        copy.start()
    for copy in copies:
        copy.wait()


def key_projection_kernel(n, table, *refs):
    chunks, (rate_ref, wide_ref, mine_kv, other_kv, x, sems) = refs[:n], refs[n:]

    @pl.when(pl.program_id(0) == 0)
    def _():
        gather_chunks(table, chunks, x, sems)

    wide = (jnp.dot(x[...], wide_ref[0], preferred_element_type=F32) * rate_ref[...]).astype(BF)
    left, right = wide[:, :HD], wide[:, HD:]
    first = table[0] == 0
    mine_kv[0] = jnp.where(first, left, right)
    other_kv[0] = jnp.where(first, right, left)


def key_projection(table, chunks, rate, wide):
    n, (rows, width) = len(chunks), chunks[0].shape
    depth = n * width
    pair = jax.ShapeDtypeStruct((2, rows, HD), BF)
    return pl.pallas_call(
        functools.partial(key_projection_kernel, n),
        grid_spec=pltpu.PrefetchScalarGridSpec(
            num_scalar_prefetch=1,
            grid=(2,),
            in_specs=[pl.BlockSpec(memory_space=pl.ANY)] * n
            + [
                pl.BlockSpec((rows, 1), lambda j, s: (0, 0)),
                pl.BlockSpec((1, depth, 2 * HD), lambda j, s: (j + 1, 0, 0)),
            ],
            out_specs=[pl.BlockSpec((1, rows, HD), lambda j, s: (j, 0, 0))] * 2,
            scratch_shapes=[pltpu.VMEM((rows, depth), BF), pltpu.SemaphoreType.DMA((n,))],
        ),
        out_shape=[pair] * 2,
        compiler_params=params(60),
        cost_estimate=cost(2 * rows * depth * 4 * HD, 2 * depth * (rows + 4 * HD)),
        name="key_projection",
    )(table, *chunks, rate, wide)


def query_projection_kernel(n, table, *refs):
    chunks, (rate_ref, wide_ref, narrow_ref, mine_q, other_q, cross_q, cross_kv, x, sems) = refs[:n], refs[n:]
    rate = rate_ref[...]

    @pl.when(pl.program_id(0) == 0)
    def _():
        gather_chunks(table, chunks, x, sems)
        wide = (jnp.dot(x[...], wide_ref[0], preferred_element_type=F32) * rate).astype(BF)
        left, right = wide[:, :HD], wide[:, HD:]
        first = table[0] == 0
        mine_q[...] = jnp.where(first, left, right)
        other_q[...] = jnp.where(first, right, left)

    @pl.when(pl.program_id(0) == 1)
    def _():
        both = jnp.concatenate((narrow_ref[1], narrow_ref[2]), axis=1)
        both = (jnp.dot(x[...], both, preferred_element_type=F32) * rate).astype(BF)
        cross_kv[0] = both[:, :HD]
        cross_kv[1] = both[:, HD:]
        cross_q[...] = (jnp.dot(x[...], narrow_ref[0], preferred_element_type=F32) * rate).astype(BF)


def query_projection(table, chunks, rate, wide, narrow):
    n, (rows, width) = len(chunks), chunks[0].shape
    depth = n * width
    one = jax.ShapeDtypeStruct((rows, HD), BF)
    held = pl.BlockSpec((rows, HD), lambda j, s: (0, 0))
    return pl.pallas_call(
        functools.partial(query_projection_kernel, n),
        grid_spec=pltpu.PrefetchScalarGridSpec(
            num_scalar_prefetch=1,
            grid=(2,),
            in_specs=[pl.BlockSpec(memory_space=pl.ANY)] * n
            + [
                pl.BlockSpec((rows, 1), lambda j, s: (0, 0)),
                pl.BlockSpec((1, depth, 2 * HD), lambda j, s: (0, 0, 0)),
                pl.BlockSpec((3, depth, HD), lambda j, s: (0, 0, 0)),
            ],
            out_specs=[held] * 3 + [pl.BlockSpec((2, rows, HD), lambda j, s: (0, 0, 0))],
            scratch_shapes=[pltpu.VMEM((rows, depth), BF), pltpu.SemaphoreType.DMA((n,))],
        ),
        out_shape=[one] * 3 + [jax.ShapeDtypeStruct((2, rows, HD), BF)],
        compiler_params=params(60),
        cost_estimate=cost(2 * rows * depth * 5 * HD, 2 * depth * (rows + 5 * HD)),
        name="query_projection",
    )(table, *chunks, rate, wide, narrow)


def pick_kernel(table, wide_kept, narrow_kept, wide_given, narrow_given, kept, given):
    kept[0, 0] = jnp.concatenate((wide_kept[...], narrow_kept[...]), axis=0)
    given[0, 0] = jnp.concatenate((wide_given[...], narrow_given[...]), axis=0)


def pick_weights(xl, wide, narrow):
    width = wide.shape[1] // 16
    depth = wide.shape[0] + narrow.shape[0]
    kept = lambda i, y, s: (0, 4 * y + 2 * s[0] + i)
    given = lambda i, y, s: (0, 4 * y + 2 * (1 - s[0]) + i)
    out = jax.ShapeDtypeStruct((2, 4, depth, width), BF)
    return pl.pallas_call(
        pick_kernel,
        grid_spec=pltpu.PrefetchScalarGridSpec(
            num_scalar_prefetch=1,
            grid=(2, 4),
            in_specs=[pl.BlockSpec((w.shape[0], width), at) for at in (kept, given) for w in (wide, narrow)],
            out_specs=[pl.BlockSpec((1, 1, depth, width), lambda i, y, s: (i, y, 0, 0))] * 2,
        ),
        out_shape=[out] * 2,
        compiler_params=params(60),
        cost_estimate=cost(0, 8 * 16 * depth * width),
        name="pick_weights",
    )(xl, wide, narrow, wide, narrow)


def audio_projection_kernel(x_ref, rate_ref, w_ref, out_ref):
    x = jnp.concatenate([x_ref[k] for k in range(x_ref.shape[0])], axis=1)
    for j in range(3):
        out_ref[j] = (jnp.dot(x, w_ref[j], preferred_element_type=F32) * rate_ref[...]).astype(BF)


def audio_projection(x, rate, w):
    parts, rows, width = x.shape
    return pl.pallas_call(
        audio_projection_kernel,
        out_shape=jax.ShapeDtypeStruct((3, rows, HD), BF),
        in_specs=[pl.BlockSpec(memory_space=pltpu.VMEM)] * 3,
        out_specs=pl.BlockSpec(memory_space=pltpu.VMEM),
        compiler_params=params(60),
        cost_estimate=cost(2 * rows * parts * width * 3 * HD, 2 * parts * width * 3 * HD),
        name="audio_projection",
    )(x, rate, w)


def softmax_step(q, pieces, state):
    scores = [lax.dot_general(q, k, NT, preferred_element_type=F32) for k, _ in pieces]
    tiles = [s[:, i : i + HD] for s in scores for i in range(0, s.shape[1], HD)]
    top = jnp.max(functools.reduce(jnp.maximum, tiles), axis=1, keepdims=True)
    if state is not None:
        top = jnp.maximum(state[0], top)
    weights = [jnp.exp2((s - top) * (SCALE * math.log2(math.e))) for s in scores]
    tiles = [w[:, i : i + HD] for w in weights for i in range(0, w.shape[1], HD)]
    total = functools.reduce(jnp.add, tiles)
    acc = functools.reduce(
        jnp.add,
        [jnp.dot(w.astype(BF), v, preferred_element_type=F32) for w, (_, v) in zip(weights, pieces)],
    )
    if state is not None:
        fade = jnp.exp2((state[0] - top) * (SCALE * math.log2(math.e)))
        total = total + state[1] * fade
        acc = acc + state[2] * fade
    return top, total, acc


def attention_kernel(n_q, n_kv, resumed, mode, *refs):
    q_refs, refs = refs[:n_q], refs[n_q:]
    kv_refs, refs = refs[:n_kv], refs[n_kv:]
    before, outs = (refs[:3], refs[3:]) if resumed else (None, refs)
    for n, q_ref in enumerate(q_refs):
        at = slice(n * q_ref.shape[0], (n + 1) * q_ref.shape[0])
        state = (before[0][at, :1], before[1][at], before[2][at]) if resumed else None
        for r in kv_refs:
            state = softmax_step(q_ref[...], [(r[0], r[1])], state)
        top, total, acc = state
        if mode == "state":
            outs[0][at] = jnp.broadcast_to(top, acc.shape)
            outs[1][at] = total
            outs[2][at] = acc
            continue
        total = jnp.sum(total, axis=1, keepdims=True)
        result = acc / total
        if mode == "merge":
            outs[0][:, : acc.shape[0] // 8, :] = result.reshape(8, -1, HD)
            logs = jnp.broadcast_to(top * SCALE + jnp.log(total), acc.shape).T[:8]
            each = acc.shape[0] // 8
            for i in range(8):
                outs[0][i, each:, :each] = logs[:, i * each : (i + 1) * each]
        else:
            outs[n][...] = result.astype(BF)


def attention(q_parts, kv_parts, state=None, mode="out", block=0, blocks=1):
    rows = q_parts[0].shape[0] // blocks
    n_q = len(q_parts)
    keys = sum(k.shape[1] for k in kv_parts)
    wide = jax.ShapeDtypeStruct((n_q * rows, HD), F32)
    whole = pl.BlockSpec(memory_space=pltpu.VMEM)
    if mode == "state":
        out_shape = [wide] * 3
    elif mode == "merge":
        out_shape = [jax.ShapeDtypeStruct((8, rows // 8 + 8, HD), F32)]
    else:
        out_shape = [jax.ShapeDtypeStruct((rows, HD), BF) for _ in q_parts]
    operands = [*q_parts, *kv_parts, *(state or ())]
    return pl.pallas_call(
        functools.partial(attention_kernel, n_q, len(kv_parts), state is not None, mode),
        grid=(1,),
        out_shape=out_shape,
        in_specs=[pl.BlockSpec((rows, HD), lambda i: (block, 0))] * n_q
        + [pl.BlockSpec(k.shape, lambda i: (0, 0, 0)) for k in kv_parts]
        + [pl.BlockSpec((n_q * rows, HD), lambda i: (0, 0)) for _ in (state or ())],
        out_specs=[pl.BlockSpec(o.shape, lambda i, n=len(o.shape): (0,) * n) for o in out_shape],
        compiler_params=params(60),
        cost_estimate=cost(8 * n_q * rows * keys * HD, 4 * (n_q * rows + keys) * HD, n_q * rows * keys),
        name="attention_" + mode,
    )(*operands)


def output_kernel(table, *refs):
    heads, weights, outs = refs[:12], refs[12:16], refs[16:]
    step = pl.program_id(0)
    first = table[2] == 0
    result = None
    for i in range(4):
        near, other, _ = heads[3 * i : 3 * i + 3]
        near, other = near[...], other[...]
        h = jnp.concatenate((jnp.where(first, near, other), jnp.where(first, other, near)), axis=1)
        term = jnp.dot(h, weights[i][0, 0, : 2 * HD], preferred_element_type=F32)
        result = term if result is None else result + term
    for i in (0, 2):
        h = jnp.concatenate((heads[3 * i + 2][...], heads[3 * i + 5][...]), axis=1)
        w = jnp.concatenate((weights[i][0, 0, 2 * HD :], weights[i + 1][0, 0, 2 * HD :]), axis=0)
        result = result + jnp.dot(h, w, preferred_element_type=F32)
    for d in range(4):

        @pl.when(step == d)
        def _():
            outs[d][...] = result.astype(outs[d].dtype)


def output_projection(table, heads, weights, block):
    rows = heads[0].shape[0]
    _, _, depth, width = weights[0].shape
    held = pl.BlockSpec((rows, HD), lambda d, s: (0, 0))
    part = pl.BlockSpec((rows, HD), lambda d, s: (block, 0))
    picked = pl.BlockSpec((1, 1, depth, width), lambda d, s: (s[1], lax.rem(s[0] + d, 4), 0, 0))
    return pl.pallas_call(
        output_kernel,
        grid_spec=pltpu.PrefetchScalarGridSpec(
            num_scalar_prefetch=1,
            grid=(4,),
            in_specs=[held, held, part] * 4 + [picked] * 4,
            out_specs=[pl.BlockSpec((rows, width), lambda d, s: (0, 0))] * 4,
        ),
        out_shape=[jax.ShapeDtypeStruct((rows, width), F32 if d == 0 else BF) for d in range(4)],
        compiler_params=params(60),
        cost_estimate=cost(2 * rows * 4 * depth * 4 * width, 2 * 16 * depth * width),
        name="output_projection",
    )(table, *heads, *weights)


def after(x, *others):
    return lax.optimization_barrier((x, *others))[0]


def scalars(*values):
    return jnp.stack([jnp.asarray(v, jnp.int32) for v in values])


def body(video, audio, video_gain, audio_gain, video_qkv, video_cross, audio_cross, video_out, cross_video_out, cross_audio_out):
    rows = video.shape[0]
    e = lax.axis_index("xh")
    y, xl, c = lax.axis_index("y"), lax.axis_index("xl"), lax.axis_index("c")

    video_wide = video.astype(F32)
    audio_wide = audio.astype(F32)
    chunk = (video_wide * video_gain).astype(BF)
    audio_scaled = (audio_wide * audio_gain).astype(BF)
    squares = jnp.concatenate((jnp.sum(video_wide * video_wide, axis=1), jnp.sum(audio_wide * audio_wide, axis=1)))

    of_x = sent_by(chunk, "xl")
    below, above = sent_by(chunk, "y", 1), sent_by(chunk, "y", 3)
    x_below, x_above = sent_by(of_x, "y", 1), sent_by(of_x, "y", 3)
    squares = sent_to_all(squares[None], HEAD)
    audio_chunks = sent_to_all(audio_scaled, HEAD)
    below = after(below, squares, audio_chunks)
    far, x_far = sent_by(below, "y", 1), sent_by(x_above, "y", 3)
    chunks, places = [], []
    for piece, dy, dx in (
        (chunk, 0, 0),
        (of_x, 0, 1),
        (below, 3, 0),
        (above, 1, 0),
        (x_below, 3, 1),
        (far, 2, 0),
        (x_above, 1, 1),
        (x_far, 2, 1),
    ):
        place = 4 * ((y + dy) % 4) + 2 * ((xl + dx) % 2)
        chunks += [piece, sent_by(piece, "c")]
        places += [place + c, place + 1 - c]
    table = scalars(e, *places)

    squares = squares.sum(axis=0).reshape(-1)
    video_rate = lax.rsqrt(squares[:rows] / video_qkv.shape[0] + EPSILON)[:, None]
    audio_rate = lax.rsqrt(squares[rows:] / audio_cross.shape[0] + EPSILON)[:, None]

    audio_mixed = audio_projection(audio_chunks, audio_rate, audio_cross.transpose(1, 0, 2))
    audio_all = sent_to_all(audio_mixed, CTX).transpose(1, 0, 2, 3).reshape(3, -1, HD)
    audio_q, audio_kv = audio_all[0], audio_all[1:]

    kept, given = pick_weights(scalars(xl), video_out, cross_video_out)
    taken = sent_by(after(given, of_x, audio_chunks), "xl")
    weights = (kept, taken, sent_by(kept, "c"), sent_by(taken, "c"))

    wide, narrow = video_qkv.transpose(1, 0, 2), video_cross.transpose(1, 0, 2)
    mine_kv, other_kv = key_projection(table, chunks, after(video_rate, audio_all), wide)
    their_kv = sent_by(other_kv, "xh")
    mine_far = [sent_by(mine_kv, "z", d) for d in (1, 3, 2)]
    their_far = [sent_by(their_kv, "z", d) for d in (1, 3, 2)]
    mine_q, other_q, cross_q, cross_kv = query_projection(table, chunks, after(video_rate, mine_kv), wide, narrow)
    their_q = sent_by(other_q, "xh")

    (merge,) = attention([audio_q], [cross_kv], None, "merge")
    merge = lax.all_to_all(merge, CTX, split_axis=0, concat_axis=0, tiled=True)
    (across,) = attention([cross_q], [audio_kv])
    across_x = sent_by(across, "xl")
    across_all = (across, across_x, sent_by(across, "c"), sent_by(across_x, "c"))

    q_parts = [mine_q, their_q]
    state = []
    for block in range(HALVES):
        state.append(
            attention(q_parts, [mine_kv, their_kv, *mine_far], None, "state", block, HALVES)
        )

    audio_rows = audio.shape[0]
    logs = merge[:, audio_rows, :audio_rows]
    share = jnp.exp(logs - jnp.max(logs, axis=0))
    share = (share / jnp.sum(share, axis=0))[:, :, None]
    audio_cross_out = jnp.sum(share * merge[:, :audio_rows], axis=0).astype(BF)
    audio_part = jnp.dot(audio_cross_out, cross_audio_out, preferred_element_type=F32).astype(BF)
    audio_part = audio_part.reshape(audio.shape[0], 16, -1).transpose(1, 0, 2)
    audio_sums = lax.all_to_all(audio_part, HEAD, split_axis=0, concat_axis=0, tiled=True)
    audio_result = (audio.astype(F32) + jnp.sum(audio_sums.astype(F32), axis=0)).astype(BF)

    results = []
    table = scalars(y, c, e)
    q_parts = list(lax.optimization_barrier((*q_parts, audio_part))[:2])
    late = after(video, *their_far)
    outs = [attention(q_parts, their_far, state[block], "out", block, HALVES) for block in range(HALVES)]
    for block, (mine, theirs) in enumerate(outs):
        near = (mine, sent_by(theirs, "xh"))
        near_x = (sent_by(mine, "xl"), lax.ppermute(theirs, ("xh", "xl"), [(i, 3 - i) for i in range(4)]))
        heads = [*near, across_all[0], *near_x, across_all[1]]
        heads += [sent_by(h, "c") for h in near] + [across_all[2]] + [sent_by(h, "c") for h in near_x] + [across_all[3]]
        parts = output_projection(table, heads, weights, block)
        total = late[block * rows // HALVES : (block + 1) * rows // HALVES].astype(F32) + parts[0]
        for d in (1, 2, 3):
            total = total + sent_by(parts[d], "y", d).astype(F32)
        results.append(total.astype(BF))
    return jnp.concatenate(results, axis=0), audio_result


def solution(mesh):
    fine = Mesh(mesh.devices.reshape(4, 2, 4, 2, 2), ("z", "xh", "y", "xl", "c"))
    return jax.shard_map(
        body,
        mesh=fine,
        in_specs=(
            P(CTX, HEAD),
            P(CTX, HEAD),
            P(HEAD),
            P(HEAD),
            P(None, None, HEAD),
            P(None, None, HEAD),
            P(None, None, HEAD),
            P(HEAD, None),
            P(HEAD, None),
            P(HEAD, None),
        ),
        out_specs=(P(CTX, HEAD), P(CTX, HEAD)),
        check_vma=False,
    )
```

```python
import functools
import math

import jax
import jax.numpy as jnp
from jax import lax
from jax.experimental import pallas as pl
from jax.experimental.pallas import tpu as pltpu
from jax.sharding import Mesh, PartitionSpec as P

HD = 128
EPSILON = 1e-06
SCALE = HD**-0.5
HEAD = ("y", "xl", "c")
CTX = ("z", "xh")
HALVES = 2
BLOCK = 384
BF = jnp.bfloat16
F32 = jnp.float32
MEGA = 1 << 20
NT = (((1,), (1,)), ((), ()))


def shift(axis, by):
    n = lax.axis_size(axis)
    return [(i, (i + by) % n) for i in range(n)]


def sent_by(x, axis, by=1):
    return lax.ppermute(x, axis, shift(axis, by))


def sent_to_all(x, axes):
    n = math.prod(lax.axis_size(a) for a in axes)
    copies = jnp.broadcast_to(x, (n, *x.shape))
    return lax.all_to_all(copies, axes, split_axis=0, concat_axis=0, tiled=True)


def for_links(shape, dtype=BF):
    return pltpu.HBM(shape, dtype)


VM = pl.BlockSpec(memory_space=pltpu.VMEM)
SM = pl.BlockSpec(memory_space=pltpu.SMEM)


def gathered_pair(x):
    return lax.all_gather(x, "c", axis=0, tiled=False)


def gathered_pairs(*values):
    return [gathered_pair(v[None]) for v in values]


def params(limit_mb):
    return pltpu.CompilerParams(vmem_limit_bytes=limit_mb * MEGA)


def cost(flops, moved, exps=0):
    return pl.CostEstimate(flops=int(flops) , bytes_accessed=int(moved), transcendentals=int(exps))


def columns_of(row):
    return jnp.broadcast_to(row, (HD, row.shape[1])).T


def multiply(x, w):
    return jnp.dot(x, w, preferred_element_type=F32)


def whole(*shape):
    return pl.BlockSpec(shape, lambda *at: (0,) * len(shape))


def rows_of(column):
    return jnp.broadcast_to(column, (column.shape[0], HD)).T[:1]


def split_terms(terms, values, stride):
    terms[...] = jnp.zeros_like(terms)
    n, width = values.shape
    for i in range(3):
        term = values.astype(BF).astype(F32)
        terms[stride * i : stride * i + n, :width] = term
        values = values - term
    return terms[...].astype(BF)


def chunk_kernel(video_ref, audio_ref, video_gain, audio_gain, video_out, audio_out, terms):
    rows, width = video_ref.shape
    audio_rows = audio_ref.shape[0]
    video = video_ref[...].astype(F32)
    video_out[:rows] = (video * video_gain[...]).astype(BF)
    row = rows_of(jnp.sum(video * video, axis=1, keepdims=True))
    sums = jnp.concatenate([row[:, i : i + width] for i in range(0, rows, width)], axis=0)
    video_out[rows:] = split_terms(terms, sums, 4)
    audio = audio_ref[...].astype(F32)
    squares = jnp.concatenate((audio * audio, jnp.zeros((HD - audio_rows, HD), F32)), axis=0)
    sums = rows_of(jnp.sum(squares, axis=1, keepdims=True))
    scaled = (audio * audio_gain[...]).astype(BF)
    split = split_terms(terms, sums, 1)[:, :HD]
    for i in range(audio_out.shape[0]):
        audio_out[i, :audio_rows] = scaled
        audio_out[i, audio_rows:] = split


def make_chunks(video, audio, video_gain, audio_gain):
    rows, width = video.shape
    shapes = [(rows + 16, width), (16, audio.shape[0] + 16, HD)]
    return pl.pallas_call(
        chunk_kernel,
        grid=(1,),
        out_shape=[for_links(s) for s in shapes],
        in_specs=[whole(*video.shape), whole(*audio.shape), whole(1, width), whole(1, HD)],
        out_specs=[whole(*s) for s in shapes],
        scratch_shapes=[pltpu.VMEM((16, width), F32)],
        compiler_params=params(60),
        cost_estimate=cost(0, 4 * rows * width),
        name="make_chunks",
    )(video, audio, video_gain[None], audio_gain[None])


def projection_kernel(n, table, *refs):
    chunks, refs = refs[:n], refs[n:]
    wide_hbm, narrow_hbm, mine_q, other_q, cross_q, mine_kv, other_kv, cross_kv, wide, narrow, sems = refs
    width = chunks[0].shape[1]
    rows = mine_q.shape[0]
    copies = [pltpu.make_async_copy(wide_hbm.at[j], wide.at[j], sems.at[j]) for j in range(3)]
    copies += [pltpu.make_async_copy(narrow_hbm.at[j], narrow.at[j], sems.at[3 + j]) for j in range(3)]
    for j in (1, 2, 0, 3, 4, 5):
        copies[j].start()
    terms = functools.reduce(jnp.add, [r[rows:].astype(F32) for r in chunks])
    rate = lax.rsqrt((terms[0:3] + terms[4:7] + terms[8:11]) / (n * width) + EPSILON)
    rate = columns_of(jnp.concatenate([rate[i : i + 1] for i in range(3)], axis=1))
    places = [pl.ds(pl.multiple_of(table[1 + k] * width, width), width) for k in range(n)]
    zero = table[0] == 0

    def weight(ref, j):
        copies[j if ref is wide else 3 + j].wait()
        return jnp.concatenate([ref[j, p] for p in places], axis=0)

    def scaled_blocks(w):
        for at in range(0, rows, BLOCK):
            block = slice(at, at + BLOCK)
            x = jnp.concatenate([r[block] for r in chunks], axis=1)
            result = multiply(x, w)
            yield block, [(result[:, i : i + HD] * rate[block]).astype(BF) for i in range(0, w.shape[1], HD)]

    for j in (1, 2, 0):
        for block, (left, right) in scaled_blocks(weight(wide, j)):
            mine, other = jnp.where(zero, left, right), jnp.where(zero, right, left)
            if j == 0:
                mine_q[block] = mine
                other_q[block] = other
            else:
                mine_kv[j - 1, block] = mine
                other_kv[j - 1, block] = other
    for block, (only,) in scaled_blocks(weight(narrow, 0)):
        cross_q[block] = only
    for block, (key, value) in scaled_blocks(jnp.concatenate((weight(narrow, 1), weight(narrow, 2)), axis=1)):
        cross_kv[0, block] = key
        cross_kv[1, block] = value


def projection(table, chunks, rows, wide, narrow):
    n, (tall, width) = len(chunks), chunks[0].shape
    depth = n * width
    one, two = (rows, HD), (2, rows, HD)
    hbm = pl.BlockSpec(memory_space=pl.ANY)
    return pl.pallas_call(
        functools.partial(projection_kernel, n),
        grid=(1,),
        in_specs=[SM] + [VM] * n + [hbm] * 2,
        out_specs=[whole(*one)] * 3 + [whole(*two)] * 3,
        scratch_shapes=[
            pltpu.VMEM((3, depth, 2 * HD), BF),
            pltpu.VMEM((3, depth, HD), BF),
            pltpu.SemaphoreType.DMA((6,)),
        ],
        out_shape=[jax.ShapeDtypeStruct(one, BF), for_links(one), jax.ShapeDtypeStruct(one, BF)]
        + [for_links(two)] * 2
        + [jax.ShapeDtypeStruct(two, BF)],
        compiler_params=params(40),
        cost_estimate=cost(2 * rows * depth * 9 * HD, 2 * depth * (rows + 9 * HD)),
        name="projection",
    )(table, *chunks, *[pltpu.with_memory_space_constraint(w, pltpu.HBM) for w in (wide, narrow)])


def audio_projection_kernel(x_ref, w_ref, out):
    audio_rows = out.shape[2]
    x = jnp.concatenate([x_ref[k, :audio_rows] for k in range(x_ref.shape[0])], axis=1)
    terms = functools.reduce(jnp.add, [x_ref[k, audio_rows:].astype(F32) for k in range(x_ref.shape[0])])
    rate = columns_of(lax.rsqrt((terms[0:1] + terms[1:2] + terms[2:3]) / x.shape[1] + EPSILON))[:audio_rows]
    for j in range(3):
        result = (multiply(x, w_ref[j]) * rate).astype(BF)
        for i in range(out.shape[0]):
            out[i, j] = result


def audio_projection(x, w):
    parts, rows, width = x.shape
    shape = (8, 3, rows - 16, HD)
    return pl.pallas_call(
        audio_projection_kernel,
        grid=(1,),
        out_shape=for_links(shape),
        in_specs=[VM] * 2,
        out_specs=pl.BlockSpec(shape, lambda i: (0, 0, 0, 0)),
        compiler_params=params(16),
        cost_estimate=cost(2 * rows * parts * width * 3 * HD, 2 * parts * width * 3 * HD),
        name="audio_projection",
    )(x, w)


def pick_kernel(table, *refs):
    blocks = [jnp.concatenate((refs[i][...], refs[i + 1][...]), axis=0) for i in range(0, 8, 2)]
    kept, kept_c, *given = refs[8:]
    kept[0] = blocks[0]
    kept_c[0] = blocks[1]
    for i in range(2):

        @pl.when(pl.program_id(0) // 2 == i)
        def _():
            given[i][0] = blocks[2]
            given[2 + i][0] = blocks[3]


def pick_weights(table, wide, narrow):
    width = wide.shape[1] // 16
    depth = wide.shape[0] + narrow.shape[0]

    def block(w, other_xl, other_c):
        def at(y, s):
            xl = 1 - s[0] if other_xl else s[0]
            c = 1 - s[1] if other_c else s[1]
            return 0, 4 * y + 2 * xl + c

        return pl.BlockSpec((w.shape[0], width), at)

    kinds = [(0, 0), (0, 1), (1, 0), (1, 1)]
    one = pl.BlockSpec((1, depth, width), lambda y, s: (y, 0, 0))
    return pl.pallas_call(
        pick_kernel,
        grid_spec=pltpu.PrefetchScalarGridSpec(
            num_scalar_prefetch=1,
            grid=(4,),
            in_specs=[block(w, *kind) for kind in kinds for w in (wide, narrow)],
            out_specs=[one] * 2
            + [
                pl.BlockSpec((1, depth, width), at)
                for at in (lambda y, s: (jnp.minimum(y, 1), 0, 0), lambda y, s: (jnp.maximum(y - 2, 0), 0, 0)) * 2
            ],
        ),
        out_shape=[for_links((4, depth, width))] * 2 + [for_links((2, depth, width))] * 4,
        compiler_params=params(60),
        cost_estimate=cost(0, 8 * 16 * depth * width),
        name="pick_weights",
    )(table, *[wide, narrow] * 4)


def softmax_step(q, pieces, state):
    scores = [lax.dot_general(q, k, NT, preferred_element_type=F32) for k, _ in pieces]
    tiles = [s[:, i : i + HD] for s in scores for i in range(0, s.shape[1], HD)]
    top = jnp.max(functools.reduce(jnp.maximum, tiles), axis=1, keepdims=True)
    if state is not None:
        top = jnp.maximum(state[0], top)
    weights = [jnp.exp2((s - top) * (SCALE * math.log2(math.e))) for s in scores]
    tiles = [w[:, i : i + HD] for w in weights for i in range(0, w.shape[1], HD)]
    total = functools.reduce(jnp.add, tiles)
    acc = functools.reduce(
        jnp.add,
        [jnp.dot(w.astype(BF), v, preferred_element_type=F32) for w, (_, v) in zip(weights, pieces)],
    )
    if state is not None:
        fade = jnp.exp2((state[0] - top) * (SCALE * math.log2(math.e)))
        total = total + state[1] * fade
        acc = acc + state[2] * fade
    return top, total, acc


def tokens_of(ref, j):
    return ref[j] if len(ref.shape) == 3 else jnp.concatenate([ref[i, j + 1] for i in range(ref.shape[0])], axis=0)


def attention_kernel(n_q, n_kv, resumed, mode, block, blocks, *refs):
    q_refs, refs = refs[:n_q], refs[n_q:]
    kv_refs, refs = refs[:n_kv], refs[n_kv:]
    before, outs, placed = None, refs, []
    if resumed:
        before, outs = refs[:2], refs[2:]
    for n, q_ref in enumerate(q_refs):
        q = tokens_of(q_ref, -1) if len(q_ref.shape) == 4 else q_ref[...]
        rows = q.shape[0] // blocks
        at = slice(n * rows, (n + 1) * rows)
        state = None
        if resumed:
            ends = before[0][at]
            state = (ends[:, :1], jnp.where(lax.broadcasted_iota(jnp.int32, ends.shape, 1) == 1, ends, 0.0), before[1][at])
        for r in kv_refs:
            state = softmax_step(q[block * rows : (block + 1) * rows], [(tokens_of(r, 0), tokens_of(r, 1))], state)
        top, total, acc = state
        total = jnp.sum(total, axis=1, keepdims=True)
        if mode == "state":
            outs[0][at] = jnp.where(lax.broadcasted_iota(jnp.int32, acc.shape, 1) == 0, top, total)
            outs[1][at] = acc
            continue
        result = acc / total
        if mode == "merge":
            each = rows // 8
            outs[0][:, :each] = result.reshape(8, -1, HD)
            logs = jnp.broadcast_to(top * SCALE + jnp.log(total), acc.shape).T[:8]
            for i in range(8):
                outs[0][i, each:, :each] = logs[:, i * each : (i + 1) * each]
        else:
            placed.append(result.astype(BF))
    for out, value in zip(outs, placed):
        out[...] = value


def attention(q_parts, kv_parts, state=None, mode="out", block=0, blocks=1):
    rows = math.prod(q_parts[0].shape[:-1:2]) // blocks
    n_q = len(q_parts)
    keys = sum(math.prod(k.shape) // (2 * HD) for k in kv_parts)
    if mode == "state":
        out_shape = [jax.ShapeDtypeStruct((n_q * rows, HD), F32)] * 2
    elif mode == "merge":
        out_shape = [for_links((8, rows // 8 + 8, HD), F32)]
    else:
        out_shape = [for_links((rows, HD)) for _ in q_parts]
    operands = [*q_parts, *kv_parts, *(state or ())]
    return pl.pallas_call(
        functools.partial(attention_kernel, n_q, len(kv_parts), state is not None, mode, block, blocks),
        grid=(1,),
        out_shape=out_shape,
        in_specs=[whole(*o.shape) if state else VM for o in operands],
        out_specs=[pl.BlockSpec(o.shape, lambda i, n=len(o.shape): (0,) * n) for o in out_shape],
        compiler_params=params(40),
        cost_estimate=cost(8 * n_q * rows * keys * HD, 4 * (n_q * rows + keys) * HD, n_q * rows * keys),
        name="attention_" + mode,
    )(*operands)


def output_kernel(block, table, heads, *refs):
    across, weights, outs = refs[:4], refs[4:10], refs[10:]
    rows, width = outs[0].shape
    at = slice(block * rows, (block + 1) * rows)
    y, first, core = table[0], table[1] == 0, table[2]
    hs = []
    for k in range(4):
        i = core if k % 2 == 0 else 1 - core
        near, other = heads[i, k // 2 * 2], heads[i, k // 2 * 2 + 1]
        hs += [jnp.where(first, near, other), jnp.where(first, other, near), across[k][at]]
    h = jnp.concatenate(hs, axis=1)

    for d in range(4):
        to = lax.rem(y + d, 4)
        low = to < 2
        half = lax.rem(to, 2)
        kept = [weights[0][to], weights[1][to]]
        taken = [jnp.where(low, weights[i][half], weights[i + 1][half]) for i in (2, 4)]
        outs[d][...] = multiply(h, jnp.concatenate(kept + taken, axis=0)).astype(outs[d].dtype)


def output_projection(table, heads, across, weights, block):
    _, _, rows, _ = heads.shape
    shape = (rows, weights[0].shape[-1])
    return pl.pallas_call(
        functools.partial(output_kernel, block),
        grid=(1,),
        out_shape=[jax.ShapeDtypeStruct(shape, F32)] + [for_links(shape)] * 3,
        in_specs=[SM] + [whole(*a.shape) for a in (heads, *across, *weights)],
        out_specs=[whole(*shape)] * 4,
        compiler_params=params(60),
        cost_estimate=cost(2 * rows * 12 * HD * 4 * shape[1], 2 * 48 * HD * shape[1]),
        name="output_projection",
    )(table, heads, *across, *weights)


def stage(*values):
    return lax.optimization_barrier(values)


def after(x, *others):
    return lax.optimization_barrier((x, *others))[0]


def scalars(*values):
    return jnp.stack([jnp.asarray(v, jnp.int32) for v in values])


def body(video, audio, video_gain, audio_gain, video_qkv, video_cross, audio_cross, video_out, cross_video_out, cross_audio_out):
    rows = video.shape[0]
    e = lax.axis_index("xh")
    y, xl, c = lax.axis_index("y"), lax.axis_index("xl"), lax.axis_index("c")

    wide, narrow, audio_w = (w.transpose(1, 0, 2) for w in (video_qkv, video_cross, audio_cross))
    order = ((0, 0), (0, 1), (3, 0), (1, 0), (3, 1), (1, 1), (2, 0), (2, 1))
    places = [4 * ((y + dy) % 4) + 2 * ((xl + dx) % 2) for dy, dx in order]
    table = scalars(e, *[p + core for p in places for core in (c, 1 - c)])

    def with_core(*chunks):
        return [a for chunk in chunks for a in (chunk, sent_by(chunk, "c"))]

    chunk, audio_copies = make_chunks(video, audio, video_gain, audio_gain)
    of_x, below, above = sent_by(chunk, "xl"), sent_by(chunk, "y", 1), sent_by(chunk, "y", 3)
    chunks = with_core(chunk)
    kept, kept_c, *given = pick_weights(scalars(xl, c), after(video_out, chunk), cross_video_out)
    of_x, below, above, kept_c, table, g_0, g_1, g_2, g_3, *chunks = stage(
        of_x, below, above, kept_c, table, *given, *chunks
    )

    x_below, x_above = sent_by(of_x, "y", 1), sent_by(of_x, "y", 3)
    audio_copies = lax.all_to_all(after(audio_copies, of_x), HEAD, split_axis=0, concat_axis=0, tiled=True)
    def from_x(x, by):
        return lax.ppermute(x, ("xh", "xl"), [(i, (i + by) % 4) for i in range(4)])

    taken_0, taken_c_0 = from_x(g_0, 1), from_x(g_2, 3)
    chunks += with_core(of_x)
    x_below, x_above, below, above, audio_copies, taken_0, taken_c_0, g_1, g_3, *chunks = stage(
        x_below, x_above, below, above, audio_copies, taken_0, taken_c_0, g_1, g_3, *chunks
    )

    far, x_far = sent_by(below, "y", 1), sent_by(x_above, "y", 3)
    taken_1, taken_c_1 = from_x(g_1, 1), from_x(g_3, 3)
    audio_mixed = audio_projection(audio_copies, audio_w)
    far, x_far, below, above, x_below, x_above, audio_mixed, taken_1, taken_c_1, *chunks = stage(
        far, x_far, below, above, x_below, x_above, audio_mixed, taken_1, taken_c_1, *chunks
    )

    audio_all = lax.all_to_all(audio_mixed, CTX, split_axis=0, concat_axis=0, tiled=True)
    chunks += with_core(below, above, x_below, x_above, far, x_far)
    kept_c = sent_by(kept_c, "c")
    kept_c, *chunks = stage(kept_c, *chunks)
    mine_q, other_q, cross_q, mine_kv, other_kv, cross_kv = projection(table, chunks, rows, wide, narrow)

    their_kv = sent_by(other_kv, "xh")
    mine_far = [sent_by(mine_kv, "z", d) for d in (1, 3, 2)]
    (merge,) = attention([audio_all], [cross_kv], None, "merge")
    (across,) = attention([cross_q], [audio_all])
    their_q = sent_by(other_q, "xh")
    merge = lax.all_to_all(merge, CTX, split_axis=0, concat_axis=0, tiled=True)
    their_kv, *mine_far, merge, across, their_q = stage(their_kv, *mine_far, merge, across, their_q)

    their_far = [sent_by(their_kv, "z", d) for d in (1, 3, 2)]
    across_x = sent_by(across, "xl")
    taken_c_0, taken_c_1 = sent_by(taken_c_0, "c"), sent_by(taken_c_1, "c")
    near_parts = [mine_kv, their_kv, *mine_far]
    states = [attention([mine_q, their_q], near_parts, None, "state", block, HALVES) for block in range(HALVES)]

    audio_rows = audio.shape[0]
    logs = merge[:, audio_rows, :audio_rows]
    share = jnp.exp(logs - jnp.max(logs, axis=0))
    share = (share / jnp.sum(share, axis=0))[:, :, None]
    audio_cross_out = jnp.sum(share * merge[:, :audio_rows], axis=0).astype(BF)
    audio_part = jnp.dot(audio_cross_out, cross_audio_out, preferred_element_type=F32).astype(BF)
    audio_part = audio_part.reshape(audio_rows, 16, -1).transpose(1, 0, 2)
    audio_sums = lax.all_to_all(audio_part, HEAD, split_axis=0, concat_axis=0, tiled=True)
    audio_sums, across, across_x, taken_c_0, taken_c_1, q_0, q_1, video, *flat = stage(
        audio_sums,
        across,
        across_x,
        taken_c_0,
        taken_c_1,
        mine_q,
        their_q,
        video,
        *states[0],
        *states[1],
        *their_far,
    )
    states, their_far = [tuple(flat[:2]), tuple(flat[2:4])], flat[4:]
    across = [across, sent_by(across, "c"), across_x, sent_by(across_x, "c")]
    weights = [kept, kept_c, taken_0, taken_1, taken_c_0, taken_c_1]
    table = scalars(y, e, c)
    step = rows // HALVES

    def finish(q, block):
        return attention([q, q_1], their_far, states[block], "out", block, HALVES)

    def spread(mine, theirs):
        across_x = lax.ppermute(theirs, ("xh", "xl"), [(i, 3 - i) for i in range(4)])
        return mine, sent_by(theirs, "xh"), sent_by(mine, "xl"), across_x

    out_0 = finish(q_0, 0)
    heads_0 = spread(*out_0)
    out_1 = finish(after(q_0, out_0[0]), 1)
    *heads_0, mine, theirs = stage(*heads_0, *out_1)
    heads_1 = spread(mine, theirs)
    parts_0 = output_projection(table, gathered_pair(jnp.stack(heads_0)), across, weights, 0)
    h_0, h_1, h_2, h_3, *parts_0 = stage(*heads_1, *parts_0)
    others_0 = [sent_by(parts_0[d], "y", d) for d in (1, 2, 3)]
    parts_1 = output_projection(table, gathered_pair(jnp.stack((h_0, h_1, h_2, h_3))), across, weights, 1)
    others_1 = [sent_by(parts_1[d], "y", d) for d in (1, 2, 3)]
    results = []
    for i, (parts, others) in enumerate(((parts_0, others_0), (parts_1, others_1))):
        total = video[i * step : (i + 1) * step].astype(F32) + parts[0]
        for other in others:
            total = total + other.astype(F32)
        results.append(total.astype(BF))
    audio_result = (audio.astype(F32) + jnp.sum(audio_sums.astype(F32), axis=0)).astype(BF)
    return jnp.concatenate(results, axis=0), audio_result


def solution(mesh):
    fine = Mesh(mesh.devices.reshape(4, 2, 4, 2, 2), ("z", "xh", "y", "xl", "c"))
    return jax.shard_map(
        body,
        mesh=fine,
        in_specs=(
            P(CTX, HEAD),
            P(CTX, HEAD),
            P(HEAD),
            P(HEAD),
            P(None, None, HEAD),
            P(None, None, HEAD),
            P(None, None, HEAD),
            P(HEAD, None),
            P(HEAD, None),
            P(HEAD, None),
        ),
        out_specs=(P(CTX, HEAD), P(CTX, HEAD)),
        check_vma=False,
    )
```

```python
import functools
import math

import jax
import jax.numpy as jnp
from jax import lax
from jax.experimental import pallas as pl
from jax.experimental.pallas import tpu as pltpu
from jax.sharding import Mesh, PartitionSpec as P

HD = 128
EPSILON = 1e-06
SCALE = HD**-0.5
HEAD = ("y", "xl", "c")
CTX = ("z", "xh")
HALVES = 2
BLOCK = 384
BF = jnp.bfloat16
F32 = jnp.float32
MEGA = 1 << 20
NT = (((1,), (1,)), ((), ()))


def shift(axis, by):
    n = lax.axis_size(axis)
    return [(i, (i + by) % n) for i in range(n)]


def sent_by(x, axis, by=1):
    return lax.ppermute(x, axis, shift(axis, by))


def sent_to_all(x, axes):
    n = math.prod(lax.axis_size(a) for a in axes)
    copies = jnp.broadcast_to(x, (n, *x.shape))
    return lax.all_to_all(copies, axes, split_axis=0, concat_axis=0, tiled=True)


def for_links(shape, dtype=BF):
    return pltpu.HBM(shape, dtype)


VM = pl.BlockSpec(memory_space=pltpu.VMEM)
SM = pl.BlockSpec(memory_space=pltpu.SMEM)


def gathered_pair(x):
    return lax.all_gather(x, "c", axis=0, tiled=False)


def gathered_pairs(*values):
    return [gathered_pair(v[None]) for v in values]


def params(limit_mb):
    return pltpu.CompilerParams(vmem_limit_bytes=limit_mb * MEGA)


def cost(flops, moved, exps=0):
    return pl.CostEstimate(flops=int(flops) , bytes_accessed=int(moved), transcendentals=int(exps))


def columns_of(row):
    return jnp.broadcast_to(row, (HD, row.shape[1])).T


def multiply(x, w):
    return jnp.dot(x, w, preferred_element_type=F32)


def whole(*shape):
    return pl.BlockSpec(shape, lambda *at: (0,) * len(shape))


def rows_of(column):
    return jnp.broadcast_to(column, (column.shape[0], HD)).T[:1]


def split_terms(terms, values, stride):
    terms[...] = jnp.zeros_like(terms)
    n, width = values.shape
    for i in range(3):
        term = values.astype(BF).astype(F32)
        terms[stride * i : stride * i + n, :width] = term
        values = values - term
    return terms[...].astype(BF)


def chunk_kernel(video_ref, audio_ref, video_gain, audio_gain, video_out, audio_out, terms):
    rows, width = video_ref.shape
    audio_rows = audio_ref.shape[0]
    video = video_ref[...].astype(F32)
    video_out[:rows] = (video * video_gain[...]).astype(BF)
    row = rows_of(jnp.sum(video * video, axis=1, keepdims=True))
    sums = jnp.concatenate([row[:, i : i + width] for i in range(0, rows, width)], axis=0)
    video_out[rows:] = split_terms(terms, sums, 4)
    audio = audio_ref[...].astype(F32)
    squares = jnp.concatenate((audio * audio, jnp.zeros((HD - audio_rows, HD), F32)), axis=0)
    sums = rows_of(jnp.sum(squares, axis=1, keepdims=True))
    scaled = (audio * audio_gain[...]).astype(BF)
    split = split_terms(terms, sums, 1)[:, :HD]
    for i in range(audio_out.shape[0]):
        audio_out[i, :audio_rows] = scaled
        audio_out[i, audio_rows:] = split


def make_chunks(video, audio, video_gain, audio_gain):
    rows, width = video.shape
    shapes = [(rows + 16, width), (16, audio.shape[0] + 16, HD)]
    return pl.pallas_call(
        chunk_kernel,
        grid=(1,),
        out_shape=[for_links(s) for s in shapes],
        in_specs=[whole(*video.shape), whole(*audio.shape), whole(1, width), whole(1, HD)],
        out_specs=[whole(*s) for s in shapes],
        scratch_shapes=[pltpu.VMEM((16, width), F32)],
        compiler_params=params(60),
        cost_estimate=cost(0, 4 * rows * width),
        name="make_chunks",
    )(video, audio, video_gain[None], audio_gain[None])


def projection_kernel(n, table, *refs):
    chunks, refs = refs[:n], refs[n:]
    wide_hbm, narrow_hbm, mine_q, other_q, cross_q, mine_kv, other_kv, cross_kv, wide, narrow, sems = refs
    width = chunks[0].shape[1]
    rows = mine_q.shape[0]
    copies = [pltpu.make_async_copy(wide_hbm.at[j], wide.at[j], sems.at[j]) for j in range(3)]
    copies += [pltpu.make_async_copy(narrow_hbm.at[j], narrow.at[j], sems.at[3 + j]) for j in range(3)]
    for j in (1, 2, 0, 3, 4, 5):
        copies[j].start()
    terms = functools.reduce(jnp.add, [r[rows:].astype(F32) for r in chunks])
    rate = lax.rsqrt((terms[0:3] + terms[4:7] + terms[8:11]) / (n * width) + EPSILON)
    rate = columns_of(jnp.concatenate([rate[i : i + 1] for i in range(3)], axis=1))
    places = [pl.ds(pl.multiple_of(table[1 + k] * width, width), width) for k in range(n)]
    zero = table[0] == 0

    def weight(ref, j):
        copies[j if ref is wide else 3 + j].wait()
        return jnp.concatenate([ref[j, p] for p in places], axis=0)

    def scaled_blocks(w):
        for at in range(0, rows, BLOCK):
            block = slice(at, at + BLOCK)
            x = jnp.concatenate([r[block] for r in chunks], axis=1)
            result = multiply(x, w)
            yield block, [(result[:, i : i + HD] * rate[block]).astype(BF) for i in range(0, w.shape[1], HD)]

    for j in (1, 2, 0):
        for block, (left, right) in scaled_blocks(weight(wide, j)):
            mine, other = jnp.where(zero, left, right), jnp.where(zero, right, left)
            if j == 0:
                mine_q[block] = mine
                other_q[block] = other
            else:
                mine_kv[j - 1, block] = mine
                other_kv[j - 1, block] = other
    for block, (only,) in scaled_blocks(weight(narrow, 0)):
        cross_q[block] = only
    for block, (key, value) in scaled_blocks(jnp.concatenate((weight(narrow, 1), weight(narrow, 2)), axis=1)):
        cross_kv[0, block] = key
        cross_kv[1, block] = value


def projection(table, chunks, rows, wide, narrow):
    n, (tall, width) = len(chunks), chunks[0].shape
    depth = n * width
    one, two = (rows, HD), (2, rows, HD)
    hbm = pl.BlockSpec(memory_space=pl.ANY)
    return pl.pallas_call(
        functools.partial(projection_kernel, n),
        grid=(1,),
        in_specs=[SM] + [VM] * n + [hbm] * 2,
        out_specs=[whole(*one)] * 3 + [whole(*two)] * 3,
        scratch_shapes=[
            pltpu.VMEM((3, depth, 2 * HD), BF),
            pltpu.VMEM((3, depth, HD), BF),
            pltpu.SemaphoreType.DMA((6,)),
        ],
        out_shape=[for_links(one)] * 3 + [for_links(two)] * 3,
        compiler_params=params(40),
        cost_estimate=cost(2 * rows * depth * 9 * HD, 2 * depth * (rows + 9 * HD)),
        name="projection",
    )(table, *chunks, *[pltpu.with_memory_space_constraint(w, pltpu.HBM) for w in (wide, narrow)])


def audio_projection_kernel(x_ref, w_ref, out):
    audio_rows = out.shape[2]
    x = jnp.concatenate([x_ref[k, :audio_rows] for k in range(x_ref.shape[0])], axis=1)
    terms = functools.reduce(jnp.add, [x_ref[k, audio_rows:].astype(F32) for k in range(x_ref.shape[0])])
    rate = columns_of(lax.rsqrt((terms[0:1] + terms[1:2] + terms[2:3]) / x.shape[1] + EPSILON))[:audio_rows]
    for j in range(3):
        result = (multiply(x, w_ref[j]) * rate).astype(BF)
        for i in range(out.shape[0]):
            out[i, j] = result


def audio_projection(x, w):
    parts, rows, width = x.shape
    shape = (8, 3, rows - 16, HD)
    return pl.pallas_call(
        audio_projection_kernel,
        grid=(1,),
        out_shape=for_links(shape),
        in_specs=[VM] * 2,
        out_specs=pl.BlockSpec(shape, lambda i: (0, 0, 0, 0)),
        compiler_params=params(16),
        cost_estimate=cost(2 * rows * parts * width * 3 * HD, 2 * parts * width * 3 * HD),
        name="audio_projection",
    )(x, w)


def pick_kernel(halves, table, *refs):
    outs = refs[4:]
    for core in range(2):
        block = jnp.concatenate((refs[2 * core][...], refs[2 * core + 1][...]), axis=0)
        for i in range(halves):

            @pl.when(pl.program_id(0) // (4 // halves) == i)
            def _():
                outs[halves * core + i][0] = block


def pick_weights(table, wide, narrow, other_xl):
    width = wide.shape[1] // 16
    depth = wide.shape[0] + narrow.shape[0]
    halves = 2 if other_xl else 1

    def block(w, other_c):
        def at(y, s):
            xl = 1 - s[0] if other_xl else s[0]
            c = 1 - s[1] if other_c else s[1]
            return 0, 4 * y + 2 * xl + c

        return pl.BlockSpec((w.shape[0], width), at)

    length = 4 // halves
    spots = [lambda y, s, i=i: (jnp.clip(y - length * i, 0, length - 1), 0, 0) for i in range(halves)]
    return pl.pallas_call(
        functools.partial(pick_kernel, halves),
        grid_spec=pltpu.PrefetchScalarGridSpec(
            num_scalar_prefetch=1,
            grid=(4,),
            in_specs=[block(w, other_c) for other_c in range(2) for w in (wide, narrow)],
            out_specs=[pl.BlockSpec((1, depth, width), at) for at in spots] * 2,
        ),
        out_shape=[for_links((length, depth, width))] * (2 * halves),
        compiler_params=params(60),
        cost_estimate=cost(0, 4 * 16 * depth * width),
        name="pick_weights",
    )(table, *[wide, narrow] * 2)


def softmax_step(q, pieces, state):
    scores = [lax.dot_general(q, k, NT, preferred_element_type=F32) for k, _ in pieces]
    tiles = [s[:, i : i + HD] for s in scores for i in range(0, s.shape[1], HD)]
    top = jnp.max(functools.reduce(jnp.maximum, tiles), axis=1, keepdims=True)
    if state is not None:
        top = jnp.maximum(state[0], top)
    weights = [jnp.exp2((s - top) * (SCALE * math.log2(math.e))) for s in scores]
    tiles = [w[:, i : i + HD] for w in weights for i in range(0, w.shape[1], HD)]
    total = functools.reduce(jnp.add, tiles)
    acc = functools.reduce(
        jnp.add,
        [jnp.dot(w.astype(BF), v, preferred_element_type=F32) for w, (_, v) in zip(weights, pieces)],
    )
    if state is not None:
        fade = jnp.exp2((state[0] - top) * (SCALE * math.log2(math.e)))
        total = total + state[1] * fade
        acc = acc + state[2] * fade
    return top, total, acc


def tokens_of(ref, j):
    return ref[j] if len(ref.shape) == 3 else jnp.concatenate([ref[i, j + 1] for i in range(ref.shape[0])], axis=0)


def attention_kernel(n_q, n_kv, resumed, mode, block, blocks, *refs):
    q_refs, refs = refs[:n_q], refs[n_q:]
    kv_refs, refs = refs[:n_kv], refs[n_kv:]
    before, outs, placed = None, refs, []
    if resumed:
        before, outs = refs[:2], refs[2:]
    for n, q_ref in enumerate(q_refs):
        q = tokens_of(q_ref, -1) if len(q_ref.shape) == 4 else q_ref[...]
        rows = q.shape[0] // blocks
        at = slice(n * rows, (n + 1) * rows)
        state = None
        if resumed:
            ends = before[0][at]
            state = (ends[:, :1], jnp.where(lax.broadcasted_iota(jnp.int32, ends.shape, 1) == 1, ends, 0.0), before[1][at])
        for r in kv_refs:
            state = softmax_step(q[block * rows : (block + 1) * rows], [(tokens_of(r, 0), tokens_of(r, 1))], state)
        top, total, acc = state
        total = jnp.sum(total, axis=1, keepdims=True)
        if mode == "state":
            outs[0][at] = jnp.where(lax.broadcasted_iota(jnp.int32, acc.shape, 1) == 0, top, total)
            outs[1][at] = acc
            continue
        result = acc / total
        if mode == "merge":
            each = rows // 8
            outs[0][:, :each] = result.reshape(8, -1, HD)
            logs = jnp.broadcast_to(top * SCALE + jnp.log(total), acc.shape).T[:8]
            for i in range(8):
                outs[0][i, each:, :each] = logs[:, i * each : (i + 1) * each]
        else:
            placed.append(result.astype(BF))
    for out, value in zip(outs, placed):
        out[...] = value


def attention(q_parts, kv_parts, state=None, mode="out", block=0, blocks=1):
    rows = math.prod(q_parts[0].shape[:-1:2]) // blocks
    n_q = len(q_parts)
    keys = sum(math.prod(k.shape) // (2 * HD) for k in kv_parts)
    if mode == "state":
        out_shape = [for_links((n_q * rows, HD), F32)] * 2
    elif mode == "merge":
        out_shape = [for_links((8, rows // 8 + 8, HD), F32)]
    else:
        out_shape = [for_links((rows, HD)) for _ in q_parts]
    operands = [*q_parts, *kv_parts, *(state or ())]
    held = state is not None or mode == "state"
    if held:
        operands = [pltpu.with_memory_space_constraint(o, pltpu.HBM) for o in operands]
    return pl.pallas_call(
        functools.partial(attention_kernel, n_q, len(kv_parts), state is not None, mode, block, blocks),
        grid=(1,),
        out_shape=out_shape,
        in_specs=[whole(*o.shape) if held else VM for o in operands],
        out_specs=[pl.BlockSpec(o.shape, lambda i, n=len(o.shape): (0,) * n) for o in out_shape],
        compiler_params=params(40),
        cost_estimate=cost(8 * n_q * rows * keys * HD, 4 * (n_q * rows + keys) * HD, n_q * rows * keys),
        name="attention_" + mode,
    )(*operands)


def output_kernel(block, table, heads, *refs):
    across, weights, outs = refs[:4], refs[4:10], refs[10:]
    rows, width = outs[0].shape
    at = slice(block * rows, (block + 1) * rows)
    y, first, core = table[0], table[1] == 0, table[2]
    hs = []
    for k in range(4):
        i = core if k % 2 == 0 else 1 - core
        near, other = heads[i, k // 2 * 2], heads[i, k // 2 * 2 + 1]
        hs += [jnp.where(first, near, other), jnp.where(first, other, near), across[k][at]]
    h = jnp.concatenate(hs, axis=1)

    for d in range(4):
        to = lax.rem(y + d, 4)
        low = to < 2
        half = lax.rem(to, 2)
        kept = [weights[0][to], weights[1][to]]
        taken = [jnp.where(low, weights[i][half], weights[i + 1][half]) for i in (2, 4)]
        outs[d][...] = multiply(h, jnp.concatenate(kept + taken, axis=0)).astype(outs[d].dtype)


def output_projection(table, heads, across, weights, block):
    _, _, rows, _ = heads.shape
    shape = (rows, weights[0].shape[-1])
    return pl.pallas_call(
        functools.partial(output_kernel, block),
        grid=(1,),
        out_shape=[jax.ShapeDtypeStruct(shape, F32)] + [for_links(shape)] * 3,
        in_specs=[SM] + [whole(*a.shape) for a in (heads, *across, *weights)],
        out_specs=[whole(*shape)] * 4,
        compiler_params=params(60),
        cost_estimate=cost(2 * rows * 12 * HD * 4 * shape[1], 2 * 48 * HD * shape[1]),
        name="output_projection",
    )(table, heads, *[pltpu.with_memory_space_constraint(a, pltpu.HBM) for a in (*across, *weights)])


def stage(*values):
    return lax.optimization_barrier(values)


def after(x, *others):
    return lax.optimization_barrier((x, *others))[0]


def scalars(*values):
    return jnp.stack([jnp.asarray(v, jnp.int32) for v in values])


def body(video, audio, video_gain, audio_gain, video_qkv, video_cross, audio_cross, video_out, cross_video_out, cross_audio_out):
    rows = video.shape[0]
    e = lax.axis_index("xh")
    y, xl, c = lax.axis_index("y"), lax.axis_index("xl"), lax.axis_index("c")

    wide, narrow, audio_w = (w.transpose(1, 0, 2) for w in (video_qkv, video_cross, audio_cross))
    order = ((0, 0), (0, 1), (3, 0), (1, 0), (3, 1), (1, 1), (2, 0), (2, 1))
    places = [4 * ((y + dy) % 4) + 2 * ((xl + dx) % 2) for dy, dx in order]
    table = scalars(e, *[p + core for p in places for core in (c, 1 - c)])

    def with_core(*chunks):
        return [a for chunk in chunks for a in (chunk, sent_by(chunk, "c"))]

    chunk, audio_copies = make_chunks(video, audio, video_gain, audio_gain)
    of_x, below, above = sent_by(chunk, "xl"), sent_by(chunk, "y", 1), sent_by(chunk, "y", 3)
    chunks = with_core(chunk)
    audio_copies = lax.all_to_all(audio_copies, HEAD, split_axis=0, concat_axis=0, tiled=True)
    spot = scalars(xl, c)
    given = pick_weights(spot, after(video_out, chunk), cross_video_out, True)
    of_x, below, above, table, g_0, g_1, g_2, g_3, *chunks = stage(of_x, below, above, table, *given, *chunks)

    x_below, x_above = sent_by(of_x, "y", 1), sent_by(of_x, "y", 3)
    def from_x(x, by):
        return lax.ppermute(x, ("xh", "xl"), [(i, (i + by) % 4) for i in range(4)])

    taken_0, taken_c_0 = from_x(g_0, 1), from_x(g_2, 3)
    chunks += with_core(of_x)
    x_below, x_above, below, above, audio_copies, taken_0, taken_c_0, g_1, g_3, *chunks = stage(
        x_below, x_above, below, above, audio_copies, taken_0, taken_c_0, g_1, g_3, *chunks
    )

    far, x_far = sent_by(below, "y", 1), sent_by(x_above, "y", 3)
    taken_1, taken_c_1 = from_x(g_1, 1), from_x(g_3, 3)
    audio_mixed = audio_projection(audio_copies, audio_w)
    kept, kept_c = pick_weights(spot, after(video_out, below), cross_video_out, False)
    far, x_far, below, above, x_below, x_above, audio_mixed, kept_c, taken_1, taken_c_1, *chunks = stage(
        far, x_far, below, above, x_below, x_above, audio_mixed, kept_c, taken_1, taken_c_1, *chunks
    )

    audio_all = lax.all_to_all(audio_mixed, CTX, split_axis=0, concat_axis=0, tiled=True)
    chunks += with_core(below, above, x_below, x_above, far, x_far)
    kept_c = sent_by(kept_c, "c")
    kept_c, *chunks = stage(kept_c, *chunks)
    mine_q, other_q, cross_q, mine_kv, other_kv, cross_kv = projection(table, chunks, rows, wide, narrow)

    their_kv = sent_by(other_kv, "xh")
    mine_far = [sent_by(mine_kv, "z", d) for d in (1, 3, 2)]
    (merge,) = attention([audio_all], [cross_kv], None, "merge")
    (across,) = attention([cross_q], [audio_all])
    their_q = sent_by(other_q, "xh")
    merge = lax.all_to_all(merge, CTX, split_axis=0, concat_axis=0, tiled=True)
    their_kv, *mine_far, merge, across, their_q = stage(their_kv, *mine_far, merge, across, their_q)

    their_far = [sent_by(their_kv, "z", d) for d in (1, 3, 2)]
    across_x = sent_by(across, "xl")
    taken_c_0, taken_c_1 = sent_by(taken_c_0, "c"), sent_by(taken_c_1, "c")
    near_parts = [mine_kv, their_kv, *mine_far]
    states = [attention([mine_q, their_q], near_parts, None, "state", block, HALVES) for block in range(HALVES)]

    audio_rows = audio.shape[0]
    logs = merge[:, audio_rows, :audio_rows]
    share = jnp.exp(logs - jnp.max(logs, axis=0))
    share = (share / jnp.sum(share, axis=0))[:, :, None]
    audio_cross_out = jnp.sum(share * merge[:, :audio_rows], axis=0).astype(BF)
    audio_part = jnp.dot(audio_cross_out, cross_audio_out, preferred_element_type=F32).astype(BF)
    audio_part = audio_part.reshape(audio_rows, 16, -1).transpose(1, 0, 2)
    audio_sums = lax.all_to_all(audio_part, HEAD, split_axis=0, concat_axis=0, tiled=True)
    audio_sums, across, across_x, taken_c_0, taken_c_1, q_0, q_1, video, *flat = stage(
        audio_sums,
        across,
        across_x,
        taken_c_0,
        taken_c_1,
        mine_q,
        their_q,
        video,
        *states[0],
        *states[1],
        *their_far,
    )
    states, their_far = [tuple(flat[:2]), tuple(flat[2:4])], flat[4:]
    across = [across, sent_by(across, "c"), across_x, sent_by(across_x, "c")]
    weights = [kept, kept_c, taken_0, taken_1, taken_c_0, taken_c_1]
    table = scalars(y, e, c)
    step = rows // HALVES

    def finish(q, block):
        return attention([q, q_1], their_far, states[block], "out", block, HALVES)

    def spread(mine, theirs):
        across_x = lax.ppermute(theirs, ("xh", "xl"), [(i, 3 - i) for i in range(4)])
        return mine, sent_by(theirs, "xh"), sent_by(mine, "xl"), across_x

    out_0 = finish(q_0, 0)
    heads_0 = spread(*out_0)
    out_1 = finish(after(q_0, out_0[0]), 1)
    *heads_0, mine, theirs = stage(*heads_0, *out_1)
    heads_1 = spread(mine, theirs)
    parts_0 = output_projection(table, gathered_pair(jnp.stack(heads_0)), across, weights, 0)
    h_0, h_1, h_2, h_3, *parts_0 = stage(*heads_1, *parts_0)
    others_0 = [sent_by(parts_0[d], "y", d) for d in (1, 2, 3)]
    parts_1 = output_projection(table, gathered_pair(jnp.stack((h_0, h_1, h_2, h_3))), across, weights, 1)
    others_1 = [sent_by(parts_1[d], "y", d) for d in (1, 2, 3)]
    results = []
    for i, (parts, others) in enumerate(((parts_0, others_0), (parts_1, others_1))):
        total = video[i * step : (i + 1) * step].astype(F32) + parts[0]
        for other in others:
            total = total + other.astype(F32)
        results.append(total.astype(BF))
    audio_result = (audio.astype(F32) + jnp.sum(audio_sums.astype(F32), axis=0)).astype(BF)
    return jnp.concatenate(results, axis=0), audio_result


def solution(mesh):
    fine = Mesh(mesh.devices.reshape(4, 2, 4, 2, 2), ("z", "xh", "y", "xl", "c"))
    return jax.shard_map(
        body,
        mesh=fine,
        in_specs=(
            P(CTX, HEAD),
            P(CTX, HEAD),
            P(HEAD),
            P(HEAD),
            P(None, None, HEAD),
            P(None, None, HEAD),
            P(None, None, HEAD),
            P(HEAD, None),
            P(HEAD, None),
            P(HEAD, None),
        ),
        out_specs=(P(CTX, HEAD), P(CTX, HEAD)),
        check_vma=False,
    )
```

```python
import functools
import math

import jax
import jax.numpy as jnp
from jax import lax
from jax.experimental import pallas as pl
from jax.experimental.pallas import tpu as pltpu
from jax.sharding import Mesh, PartitionSpec as P

HD = 128
EPSILON = 1e-06
SCALE = HD**-0.5
HEAD = ("y", "xl", "c")
CTX = ("z", "xh")
HALVES = 2
BLOCK = 384
BF = jnp.bfloat16
F32 = jnp.float32
MEGA = 1 << 20
NT = (((1,), (1,)), ((), ()))


def shift(axis, by):
    n = lax.axis_size(axis)
    return [(i, (i + by) % n) for i in range(n)]


def sent_by(x, axis, by=1):
    return lax.ppermute(x, axis, shift(axis, by))


def sent_to_all(x, axes):
    n = math.prod(lax.axis_size(a) for a in axes)
    copies = jnp.broadcast_to(x, (n, *x.shape))
    return lax.all_to_all(copies, axes, split_axis=0, concat_axis=0, tiled=True)


def for_links(shape, dtype=BF):
    return pltpu.HBM(shape, dtype)


VM = pl.BlockSpec(memory_space=pltpu.VMEM)
SM = pl.BlockSpec(memory_space=pltpu.SMEM)


def gathered_pair(x):
    return lax.all_gather(x, "c", axis=0, tiled=False)


def gathered_pairs(*values):
    return [gathered_pair(v[None]) for v in values]


def params(limit_mb):
    return pltpu.CompilerParams(vmem_limit_bytes=limit_mb * MEGA)


def cost(flops, moved, exps=0):
    return pl.CostEstimate(flops=int(flops) , bytes_accessed=int(moved), transcendentals=int(exps))


def columns_of(row):
    return jnp.broadcast_to(row, (HD, row.shape[1])).T


def multiply(x, w):
    return jnp.dot(x, w, preferred_element_type=F32)


def whole(*shape):
    return pl.BlockSpec(shape, lambda *at: (0,) * len(shape))


def rows_of(column):
    return jnp.broadcast_to(column, (column.shape[0], HD)).T[:1]


def split_terms(terms, values, stride):
    terms[...] = jnp.zeros_like(terms)
    n, width = values.shape
    for i in range(3):
        term = values.astype(BF).astype(F32)
        terms[stride * i : stride * i + n, :width] = term
        values = values - term
    return terms[...].astype(BF)


def chunk_kernel(video_ref, audio_ref, video_gain, audio_gain, video_out, audio_out, terms):
    rows, width = video_ref.shape
    audio_rows = audio_ref.shape[0]
    video = video_ref[...].astype(F32)
    video_out[:rows] = (video * video_gain[...]).astype(BF)
    row = rows_of(jnp.sum(video * video, axis=1, keepdims=True))
    sums = jnp.concatenate([row[:, i : i + width] for i in range(0, rows, width)], axis=0)
    video_out[rows:] = split_terms(terms, sums, 4)
    audio = audio_ref[...].astype(F32)
    squares = jnp.concatenate((audio * audio, jnp.zeros((HD - audio_rows, HD), F32)), axis=0)
    sums = rows_of(jnp.sum(squares, axis=1, keepdims=True))
    scaled = (audio * audio_gain[...]).astype(BF)
    split = split_terms(terms, sums, 1)[:, :HD]
    for i in range(audio_out.shape[0]):
        audio_out[i, :audio_rows] = scaled
        audio_out[i, audio_rows:] = split


def make_chunks(video, audio, video_gain, audio_gain):
    rows, width = video.shape
    shapes = [(rows + 16, width), (16, audio.shape[0] + 16, HD)]
    return pl.pallas_call(
        chunk_kernel,
        grid=(1,),
        out_shape=[for_links(s) for s in shapes],
        in_specs=[whole(*video.shape), whole(*audio.shape), whole(1, width), whole(1, HD)],
        out_specs=[whole(*s) for s in shapes],
        scratch_shapes=[pltpu.VMEM((16, width), F32)],
        compiler_params=params(60),
        cost_estimate=cost(0, 4 * rows * width),
        name="make_chunks",
    )(video, audio, video_gain[None], audio_gain[None])


def projection_kernel(n, table, *refs):
    chunks, refs = refs[:n], refs[n:]
    wide_hbm, narrow_hbm, mine_q, other_q, cross_q, mine_kv, other_kv, cross_kv, wide, narrow, sems = refs
    width = chunks[0].shape[1]
    rows = mine_q.shape[0]
    copies = [pltpu.make_async_copy(wide_hbm.at[j], wide.at[j], sems.at[j]) for j in range(3)]
    copies += [pltpu.make_async_copy(narrow_hbm.at[j], narrow.at[j], sems.at[3 + j]) for j in range(3)]
    for j in (1, 2, 0, 3, 4, 5):
        copies[j].start()
    terms = functools.reduce(jnp.add, [r[rows:].astype(F32) for r in chunks])
    rate = lax.rsqrt((terms[0:3] + terms[4:7] + terms[8:11]) / (n * width) + EPSILON)
    rate = columns_of(jnp.concatenate([rate[i : i + 1] for i in range(3)], axis=1))
    places = [pl.ds(pl.multiple_of(table[1 + k] * width, width), width) for k in range(n)]
    zero = table[0] == 0

    def weight(ref, j):
        copies[j if ref is wide else 3 + j].wait()
        return jnp.concatenate([ref[j, p] for p in places], axis=0)

    def scaled_blocks(w):
        for at in range(0, rows, BLOCK):
            block = slice(at, at + BLOCK)
            x = jnp.concatenate([r[block] for r in chunks], axis=1)
            result = multiply(x, w)
            yield block, [(result[:, i : i + HD] * rate[block]).astype(BF) for i in range(0, w.shape[1], HD)]

    for j in (1, 2, 0):
        for block, (left, right) in scaled_blocks(weight(wide, j)):
            mine, other = jnp.where(zero, left, right), jnp.where(zero, right, left)
            if j == 0:
                mine_q[block] = mine
                other_q[block] = other
            else:
                mine_kv[j - 1, block] = mine
                other_kv[j - 1, block] = other
    for block, (only,) in scaled_blocks(weight(narrow, 0)):
        cross_q[block] = only
    for block, (key, value) in scaled_blocks(jnp.concatenate((weight(narrow, 1), weight(narrow, 2)), axis=1)):
        cross_kv[0, block] = key
        cross_kv[1, block] = value


def projection(table, chunks, rows, wide, narrow):
    n, (tall, width) = len(chunks), chunks[0].shape
    depth = n * width
    one, two = (rows, HD), (2, rows, HD)
    hbm = pl.BlockSpec(memory_space=pl.ANY)
    return pl.pallas_call(
        functools.partial(projection_kernel, n),
        grid=(1,),
        in_specs=[SM] + [VM] * n + [hbm] * 2,
        out_specs=[whole(*one)] * 3 + [whole(*two)] * 3,
        scratch_shapes=[
            pltpu.VMEM((3, depth, 2 * HD), BF),
            pltpu.VMEM((3, depth, HD), BF),
            pltpu.SemaphoreType.DMA((6,)),
        ],
        out_shape=[for_links(one)] * 3 + [for_links(two)] * 3,
        compiler_params=params(40),
        cost_estimate=cost(2 * rows * depth * 9 * HD, 2 * depth * (rows + 9 * HD)),
        name="projection",
    )(table, *chunks, *[pltpu.with_memory_space_constraint(w, pltpu.HBM) for w in (wide, narrow)])


def audio_projection_kernel(x_ref, w_ref, out):
    audio_rows = out.shape[2]
    x = jnp.concatenate([x_ref[k, :audio_rows] for k in range(x_ref.shape[0])], axis=1)
    terms = functools.reduce(jnp.add, [x_ref[k, audio_rows:].astype(F32) for k in range(x_ref.shape[0])])
    rate = columns_of(lax.rsqrt((terms[0:1] + terms[1:2] + terms[2:3]) / x.shape[1] + EPSILON))[:audio_rows]
    for j in range(3):
        result = (multiply(x, w_ref[j]) * rate).astype(BF)
        for i in range(out.shape[0]):
            out[i, j] = result


def audio_projection(x, w):
    parts, rows, width = x.shape
    shape = (8, 3, rows - 16, HD)
    return pl.pallas_call(
        audio_projection_kernel,
        grid=(1,),
        out_shape=for_links(shape),
        in_specs=[VM] * 2,
        out_specs=pl.BlockSpec(shape, lambda i: (0, 0, 0, 0)),
        compiler_params=params(16),
        cost_estimate=cost(2 * rows * parts * width * 3 * HD, 2 * parts * width * 3 * HD),
        name="audio_projection",
    )(x, w)


def pick_kernel(halves, table, *refs):
    outs = refs[4:]
    for core in range(2):
        block = jnp.concatenate((refs[2 * core][...], refs[2 * core + 1][...]), axis=0)
        for i in range(halves):

            @pl.when(pl.program_id(0) // (4 // halves) == i)
            def _():
                outs[halves * core + i][0] = block


def pick_weights(table, wide, narrow, other_xl):
    width = wide.shape[1] // 16
    depth = wide.shape[0] + narrow.shape[0]
    halves = 2 if other_xl else 1

    def block(w, other_c):
        def at(y, s):
            xl = 1 - s[0] if other_xl else s[0]
            c = 1 - s[1] if other_c else s[1]
            return 0, 4 * y + 2 * xl + c

        return pl.BlockSpec((w.shape[0], width), at)

    length = 4 // halves
    spots = [lambda y, s, i=i: (jnp.clip(y - length * i, 0, length - 1), 0, 0) for i in range(halves)]
    return pl.pallas_call(
        functools.partial(pick_kernel, halves),
        grid_spec=pltpu.PrefetchScalarGridSpec(
            num_scalar_prefetch=1,
            grid=(4,),
            in_specs=[block(w, other_c) for other_c in range(2) for w in (wide, narrow)],
            out_specs=[pl.BlockSpec((1, depth, width), at) for at in spots] * 2,
        ),
        out_shape=[for_links((length, depth, width))] * (2 * halves),
        compiler_params=params(60),
        cost_estimate=cost(0, 4 * 16 * depth * width),
        name="pick_weights",
    )(table, *[wide, narrow] * 2)


def softmax_step(q, pieces, state):
    scores = [lax.dot_general(q, k, NT, preferred_element_type=F32) for k, _ in pieces]
    tiles = [s[:, i : i + HD] for s in scores for i in range(0, s.shape[1], HD)]
    top = jnp.max(functools.reduce(jnp.maximum, tiles), axis=1, keepdims=True)
    if state is not None:
        top = jnp.maximum(state[0], top)
    weights = [jnp.exp2((s - top) * (SCALE * math.log2(math.e))) for s in scores]
    tiles = [w[:, i : i + HD] for w in weights for i in range(0, w.shape[1], HD)]
    total = functools.reduce(jnp.add, tiles)
    acc = functools.reduce(
        jnp.add,
        [jnp.dot(w.astype(BF), v, preferred_element_type=F32) for w, (_, v) in zip(weights, pieces)],
    )
    if state is not None:
        fade = jnp.exp2((state[0] - top) * (SCALE * math.log2(math.e)))
        total = total + state[1] * fade
        acc = acc + state[2] * fade
    return top, total, acc


def tokens_of(ref, j):
    return ref[j] if len(ref.shape) == 3 else jnp.concatenate([ref[i, j + 1] for i in range(ref.shape[0])], axis=0)


def attention_kernel(n_q, n_kv, resumed, mode, block, blocks, *refs):
    q_refs, refs = refs[:n_q], refs[n_q:]
    kv_refs, refs = refs[:n_kv], refs[n_kv:]
    before, outs, placed = None, refs, []
    if resumed:
        before, outs = refs[:2], refs[2:]
    for n, q_ref in enumerate(q_refs):
        q = tokens_of(q_ref, -1) if len(q_ref.shape) == 4 else q_ref[...]
        rows = q.shape[0] // blocks
        at = slice(n * rows, (n + 1) * rows)
        state = None
        if resumed:
            ends = before[0][at]
            state = (ends[:, :1], jnp.where(lax.broadcasted_iota(jnp.int32, ends.shape, 1) == 1, ends, 0.0), before[1][at])
        for r in kv_refs:
            state = softmax_step(q[block * rows : (block + 1) * rows], [(tokens_of(r, 0), tokens_of(r, 1))], state)
        top, total, acc = state
        total = jnp.sum(total, axis=1, keepdims=True)
        if mode == "state":
            outs[0][at] = jnp.where(lax.broadcasted_iota(jnp.int32, acc.shape, 1) == 0, top, total)
            outs[1][at] = acc
            continue
        result = acc / total
        if mode == "merge":
            each = rows // 8
            outs[0][:, :each] = result.reshape(8, -1, HD)
            logs = jnp.broadcast_to(top * SCALE + jnp.log(total), acc.shape).T[:8]
            for i in range(8):
                outs[0][i, each:, :each] = logs[:, i * each : (i + 1) * each]
        else:
            placed.append(result.astype(BF))
    for out, value in zip(outs, placed):
        out[...] = value


def attention(q_parts, kv_parts, state=None, mode="out", block=0, blocks=1):
    rows = math.prod(q_parts[0].shape[:-1:2]) // blocks
    n_q = len(q_parts)
    keys = sum(math.prod(k.shape) // (2 * HD) for k in kv_parts)
    if mode == "state":
        out_shape = [for_links((n_q * rows, HD), F32)] * 2
    elif mode == "merge":
        out_shape = [for_links((8, rows // 8 + 8, HD), F32)]
    else:
        out_shape = [for_links((rows, HD)) for _ in q_parts]
    operands = [*q_parts, *kv_parts, *(state or ())]
    held = state is not None or mode == "state"
    if held:
        operands = [pltpu.with_memory_space_constraint(o, pltpu.HBM) for o in operands]
    return pl.pallas_call(
        functools.partial(attention_kernel, n_q, len(kv_parts), state is not None, mode, block, blocks),
        grid=(1,),
        out_shape=out_shape,
        in_specs=[whole(*o.shape) if held else VM for o in operands],
        out_specs=[pl.BlockSpec(o.shape, lambda i, n=len(o.shape): (0,) * n) for o in out_shape],
        compiler_params=params(40),
        cost_estimate=cost(8 * n_q * rows * keys * HD, 4 * (n_q * rows + keys) * HD, n_q * rows * keys),
        name="attention_" + mode,
    )(*operands)


def output_kernel(table, heads, *refs):
    across, weights, outs = refs[:4], refs[4:10], refs[10:]
    rows, width = outs[0].shape
    y, first, core = table[0], table[1] == 0, table[2]
    hs = []
    for k in range(4):
        i = core if k % 2 == 0 else 1 - core
        near, other = heads[i, k // 2 * 2], heads[i, k // 2 * 2 + 1]
        hs += [jnp.where(first, near, other), jnp.where(first, other, near), across[k][...]]
    h = jnp.concatenate(hs, axis=1)

    for d in range(4):
        to = lax.rem(y + d, 4)
        low = to < 2
        half = lax.rem(to, 2)
        kept = [weights[0][to], weights[1][to]]
        taken = [jnp.where(low, weights[i][half], weights[i + 1][half]) for i in (2, 4)]
        outs[d][...] = multiply(h, jnp.concatenate(kept + taken, axis=0)).astype(outs[d].dtype)


def output_projection(table, heads, across, weights, block):
    _, _, rows, _ = heads.shape
    shape = (rows, weights[0].shape[-1])
    return pl.pallas_call(
        output_kernel,
        grid=(1,),
        out_shape=[jax.ShapeDtypeStruct(shape, F32)] + [for_links(shape)] * 3,
        in_specs=[SM, whole(*heads.shape)]
        + [pl.BlockSpec((rows, HD), lambda i: (block, 0))] * 4
        + [whole(*w.shape) for w in weights],
        out_specs=[whole(*shape)] * 4,
        compiler_params=params(60),
        cost_estimate=cost(2 * rows * 12 * HD * 4 * shape[1], 2 * 48 * HD * shape[1]),
        name="output_projection",
    )(table, heads, *[pltpu.with_memory_space_constraint(a, pltpu.HBM) for a in (*across, *weights)])


def stage(*values):
    return lax.optimization_barrier(values)


def after(x, *others):
    return lax.optimization_barrier((x, *others))[0]


def scalars(*values):
    return jnp.stack([jnp.asarray(v, jnp.int32) for v in values])


def body(video, audio, video_gain, audio_gain, video_qkv, video_cross, audio_cross, video_out, cross_video_out, cross_audio_out):
    rows = video.shape[0]
    e = lax.axis_index("xh")
    y, xl, c = lax.axis_index("y"), lax.axis_index("xl"), lax.axis_index("c")

    wide, narrow, audio_w = (w.transpose(1, 0, 2) for w in (video_qkv, video_cross, audio_cross))
    order = ((0, 0), (0, 1), (3, 0), (1, 0), (3, 1), (1, 1), (2, 0), (2, 1))
    places = [4 * ((y + dy) % 4) + 2 * ((xl + dx) % 2) for dy, dx in order]
    table = scalars(e, *[p + core for p in places for core in (c, 1 - c)])

    def with_core(*chunks):
        return [a for chunk in chunks for a in (chunk, sent_by(chunk, "c"))]

    chunk, audio_copies = make_chunks(video, audio, video_gain, audio_gain)
    of_x, below, above = sent_by(chunk, "xl"), sent_by(chunk, "y", 1), sent_by(chunk, "y", 3)
    chunks = with_core(chunk)
    audio_copies = lax.all_to_all(audio_copies, HEAD, split_axis=0, concat_axis=0, tiled=True)
    spot = scalars(xl, c)
    given = pick_weights(spot, after(video_out, chunk), cross_video_out, True)
    of_x, below, above, table, g_0, g_1, g_2, g_3, *chunks = stage(of_x, below, above, table, *given, *chunks)

    x_below, x_above = sent_by(of_x, "y", 1), sent_by(of_x, "y", 3)
    def from_x(x, by):
        return lax.ppermute(x, ("xh", "xl"), [(i, (i + by) % 4) for i in range(4)])

    taken_0, taken_c_0 = from_x(g_0, 1), from_x(g_2, 3)
    chunks += with_core(of_x)
    x_below, x_above, below, above, audio_copies, taken_0, taken_c_0, g_1, g_3, *chunks = stage(
        x_below, x_above, below, above, audio_copies, taken_0, taken_c_0, g_1, g_3, *chunks
    )

    far, x_far = sent_by(below, "y", 1), sent_by(x_above, "y", 3)
    taken_1, taken_c_1 = from_x(g_1, 1), from_x(g_3, 3)
    audio_mixed = audio_projection(audio_copies, audio_w)
    kept, kept_c = pick_weights(spot, after(video_out, below), cross_video_out, False)
    far, x_far, below, above, x_below, x_above, audio_mixed, kept_c, taken_1, taken_c_1, *chunks = stage(
        far, x_far, below, above, x_below, x_above, audio_mixed, kept_c, taken_1, taken_c_1, *chunks
    )

    audio_all = lax.all_to_all(audio_mixed, CTX, split_axis=0, concat_axis=0, tiled=True)
    chunks += with_core(below, above, x_below, x_above, far, x_far)
    kept_c = sent_by(kept_c, "c")
    kept_c, *chunks = stage(kept_c, *chunks)
    mine_q, other_q, cross_q, mine_kv, other_kv, cross_kv = projection(table, chunks, rows, wide, narrow)

    their_kv = sent_by(other_kv, "xh")
    mine_far = [sent_by(mine_kv, "z", d) for d in (1, 3, 2)]
    (merge,) = attention([audio_all], [cross_kv], None, "merge")
    (across,) = attention([cross_q], [audio_all])
    their_q = sent_by(other_q, "xh")
    merge = lax.all_to_all(merge, CTX, split_axis=0, concat_axis=0, tiled=True)
    their_kv, *mine_far, merge, across, their_q = stage(their_kv, *mine_far, merge, across, their_q)

    their_far = [sent_by(their_kv, "z", d) for d in (1, 3, 2)]
    across_x = sent_by(across, "xl")
    taken_c_0, taken_c_1 = sent_by(taken_c_0, "c"), sent_by(taken_c_1, "c")
    near_parts = [mine_kv, their_kv, *mine_far]
    states = [attention([mine_q, their_q], near_parts, None, "state", block, HALVES) for block in range(HALVES)]

    audio_rows = audio.shape[0]
    logs = merge[:, audio_rows, :audio_rows]
    share = jnp.exp(logs - jnp.max(logs, axis=0))
    share = (share / jnp.sum(share, axis=0))[:, :, None]
    audio_cross_out = jnp.sum(share * merge[:, :audio_rows], axis=0).astype(BF)
    audio_part = jnp.dot(audio_cross_out, cross_audio_out, preferred_element_type=F32).astype(BF)
    audio_part = audio_part.reshape(audio_rows, 16, -1).transpose(1, 0, 2)
    audio_sums = lax.all_to_all(audio_part, HEAD, split_axis=0, concat_axis=0, tiled=True)
    audio_sums, across, across_x, taken_c_0, taken_c_1, q_0, q_1, video, *flat = stage(
        audio_sums,
        across,
        across_x,
        taken_c_0,
        taken_c_1,
        mine_q,
        their_q,
        video,
        *states[0],
        *states[1],
        *their_far,
    )
    states, their_far = [tuple(flat[:2]), tuple(flat[2:4])], flat[4:]
    across = [across, sent_by(across, "c"), across_x, sent_by(across_x, "c")]
    weights = [kept, kept_c, taken_0, taken_1, taken_c_0, taken_c_1]
    table = scalars(y, e, c)
    step = rows // HALVES

    def finish(q, block):
        return attention([q, q_1], their_far, states[block], "out", block, HALVES)

    def spread(mine, theirs):
        across_x = lax.ppermute(theirs, ("xh", "xl"), [(i, 3 - i) for i in range(4)])
        return mine, sent_by(theirs, "xh"), sent_by(mine, "xl"), across_x

    out_0 = finish(q_0, 0)
    heads_0 = spread(*out_0)
    out_1 = finish(after(q_0, out_0[0]), 1)
    *heads_0, mine, theirs = stage(*heads_0, *out_1)
    heads_1 = spread(mine, theirs)
    parts_0 = output_projection(table, gathered_pair(jnp.stack(heads_0)), across, weights, 0)
    h_0, h_1, h_2, h_3, *parts_0 = stage(*heads_1, *parts_0)
    others_0 = [sent_by(parts_0[d], "y", d) for d in (1, 2, 3)]
    parts_1 = output_projection(table, gathered_pair(jnp.stack((h_0, h_1, h_2, h_3))), across, weights, 1)
    others_1 = [sent_by(parts_1[d], "y", d) for d in (1, 2, 3)]
    results = []
    for i, (parts, others) in enumerate(((parts_0, others_0), (parts_1, others_1))):
        total = video[i * step : (i + 1) * step].astype(F32) + parts[0]
        for other in others:
            total = total + other.astype(F32)
        results.append(total.astype(BF))
    audio_result = (audio.astype(F32) + jnp.sum(audio_sums.astype(F32), axis=0)).astype(BF)
    return jnp.concatenate(results, axis=0), audio_result


def solution(mesh):
    fine = Mesh(mesh.devices.reshape(4, 2, 4, 2, 2), ("z", "xh", "y", "xl", "c"))
    return jax.shard_map(
        body,
        mesh=fine,
        in_specs=(
            P(CTX, HEAD),
            P(CTX, HEAD),
            P(HEAD),
            P(HEAD),
            P(None, None, HEAD),
            P(None, None, HEAD),
            P(None, None, HEAD),
            P(HEAD, None),
            P(HEAD, None),
            P(HEAD, None),
        ),
        out_specs=(P(CTX, HEAD), P(CTX, HEAD)),
        check_vma=False,
    )
```
